32 devices in a mesh: occ: 4 (over z), pan: 8 (over y, x, core).
Axes of the slice: x: 2, y: 2, z: 4, core: 2. Of those that a mesh axis runs over, the one named last changes fastest.
Arguments:
- gamma_ia: bfloat16 [2, 1024, 8704], P(None, 'occ', 'pan'), may hold values from -6 to 6
- coef_virt: bfloat16 [10240, 8704], P(None, 'pan'), may hold values from -0.09375 to 0.09375
- coef_occ: bfloat16 [10240, 1024], P('occ'), may hold values from -0.1875 to 0.1875
- tile_mask: int32 [80, 80], replicated, may hold values from 0 to 1, as said below
- tile_owner: int32 [80, 80], replicated, may hold values from 0 to 7, as said below
Outputs:
- gradient_tiles: bfloat16 [4, 8, 8, 2, 2, 128, 128], P('occ', 'pan')
The draws below stay inside these ranges and needn't reach their ends.
Inputs may be any that keep to these rules, and one draw needn't show every extreme that they name: `tile_mask`: each block of 20 x 10 tiles holds at most 16 ones. `tile_owner`: within each block of 20 x 10 tiles, at most 2 tiles with tile_mask 1 share an owner; in every draw some block gives exactly 2 such tiles to one owner.
All inputs are finite; a program needn't handle non-finite values.
Results may differ from the reference program's by a relative error of at most 0.005.
Values may be sent and summed in bfloat16 or wider, within the bound.
A program may use at most 128 MiB of HBM per device.

```python
import jax
import jax.numpy as jnp
from jax import lax

NOCC = 1024
NVIR = 8704
NAO = 10240
AUX = 2
TILE = 128
SCAP = 2
NT = 80
MT = 20
NTP = 10
OWNERS = 8
N_OCC = 4
N_PAN = 8


def tile_pattern(key):
    base = jax.random.fold_in(key, 913)
    first = jax.random.fold_in(base, 1)
    second = jax.random.fold_in(base, 2)
    third = jax.random.fold_in(base, 3)
    fourth = jax.random.fold_in(base, 4)
    row_index = lax.broadcasted_iota(jnp.int32, (NT, NT), 0)
    col_index = lax.broadcasted_iota(jnp.int32, (NT, NT), 1)
    spacing = jnp.abs(row_index - col_index)
    limit = jnp.maximum(150, 850 - 25 * spacing)
    screened = (jax.random.randint(first, (NT, NT), 0, 1000) < limit) | (row_index < MT) & (col_index < NTP)
    scores = jax.random.randint(second, (NT, NT), 0, 4096) * (NT * NT) + row_index * NT + col_index
    ordered = jnp.where(screened, scores, scores + 4096 * NT * NT)
    row_blocks = NT // MT
    col_blocks = NT // NTP
    blocked = ordered.reshape(row_blocks, MT, col_blocks, NTP).transpose(0, 2, 1, 3).reshape(row_blocks, col_blocks, MT * NTP)
    places = jnp.argsort(jnp.argsort(blocked, axis=-1), axis=-1).astype(jnp.int32)
    places = places.reshape(row_blocks, col_blocks, MT, NTP).transpose(0, 2, 1, 3).reshape(NT, NT)
    kept = screened & (places < OWNERS * SCAP)
    turns = jax.random.randint(third, (row_blocks, col_blocks), 0, OWNERS)
    turns = jnp.repeat(jnp.repeat(turns, MT, axis=0), NTP, axis=1)
    stray = jax.random.randint(fourth, (NT, NT), 0, OWNERS)
    owners_of = jnp.where(kept, (places + turns) % OWNERS, stray).astype(jnp.int32)
    return (kept.astype(jnp.int32), owners_of)


def draw_tile_mask(key, part):
    return tile_pattern(key)[0]


def draw_tile_owner(key, part):
    return tile_pattern(key)[1]


def strengthened(array, stream_key, source, target, parts, factor):
    def block_of(axis_at):
        return (jnp.arange(array.shape[axis_at]) // (array.shape[axis_at] // parts)).reshape((-1,) + (1,) * (array.ndim - 1 - axis_at))

    first = jax.random.permutation(stream_key, parts)[block_of(target)]
    other_side = (block_of(target) + parts // 2) % parts
    return jnp.where((block_of(source) == first) | (block_of(source) == other_side), factor * array, array)


def steps_of(key, dims, shards, smallest, largest):
    loudness = 1.0
    for axis_at, shards_of in shards:
        steps = jax.random.uniform(jax.random.fold_in(jax.random.fold_in(key, 6), axis_at), (shards_of,), jnp.float32, smallest / len(shards), largest / len(shards))
        loudness = loudness * jnp.repeat(jnp.exp(steps), dims[axis_at] // shards_of).reshape((-1,) + (1,) * (len(dims) - 1 - axis_at))
    return loudness


def scatter_about(own_key, extent, spread, reach, split=(), held_as=jnp.bfloat16):
    gain = steps_of(own_key, extent, split, -0.22, 0.18) if split else 1.0
    drawn = jax.random.normal(own_key, extent, jnp.float32) * spread * gain
    return jnp.minimum(jnp.maximum(drawn, -reach), reach).astype(held_as)


def gaussian_with(key, extent, scale, bound, shards, heavy, held_as=jnp.bfloat16):
    result = scale * jax.random.normal(key, extent, jnp.float32)
    if shards:
        result = result * steps_of(key, extent, shards, -0.22, 0.18)
    return jnp.clip(strengthened(result, jax.random.fold_in(key, 3), *heavy), -bound, bound).astype(held_as)


def setup_inputs(seed: int = 0) -> dict:
    arg_keys = jax.random.split(jax.random.key(seed), 6)
    gamma_ia = scatter_about(arg_keys[0], (AUX, NOCC, NVIR), 1.0, 6.0, ((1, 4), (2, 8)))
    coef_virt = gaussian_with(arg_keys[1], (NAO, NVIR), NVIR ** -0.5, 0.09375, ((1, 8),), (1, 0, 8, 2.0))
    coef_occ = scatter_about(arg_keys[2], (NAO, NOCC), NOCC ** -0.5, 0.1875, ((0, 4),))
    tile_mask = draw_tile_mask(jax.random.fold_in(arg_keys[5], 71), 0)
    tile_owner = draw_tile_owner(jax.random.fold_in(arg_keys[5], 71), 0)
    return {"gamma_ia": gamma_ia, "coef_virt": coef_virt, "coef_occ": coef_occ, "tile_mask": tile_mask, "tile_owner": tile_owner}


def route_slots(block_mask, block_owner, owners):
    usable = block_mask.reshape(-1)
    owners_of = block_owner.reshape(-1)
    belongs = ((usable[:, None] == 1) & (owners_of[:, None] == jnp.arange(owners, dtype=jnp.int32)[None, :])).astype(jnp.int32)
    order_rank = jnp.cumsum(belongs, axis=0) - belongs
    matched = belongs[:, :, None] * (order_rank[:, :, None] == jnp.arange(SCAP, dtype=jnp.int32)[None, None, :]).astype(jnp.int32)
    tile_index = jnp.arange(usable.shape[0], dtype=jnp.int32)
    slot_tile = jnp.sum(matched * tile_index[:, None, None], axis=0).astype(jnp.int32)
    filled = jnp.sum(matched, axis=0)
    return slot_tile, filled


def reference(gamma_ia, coef_virt, coef_occ, tile_mask, tile_owner):
    gamma_flat = gamma_ia.reshape(AUX * NOCC, NVIR)
    half_x = lax.dot_general(gamma_flat, coef_virt, (((1,), (1,)), ((), ())), preferred_element_type=jnp.float32)
    half_x = half_x.astype(jnp.bfloat16).reshape(AUX, NOCC, NAO)

    def one_block(block_id):
        row_block = block_id // N_PAN
        col_block = block_id % N_PAN
        row_coef = lax.dynamic_slice(coef_occ, ((row_block * MT * TILE).astype(jnp.int32), jnp.int32(0)), (MT * TILE, NOCC))
        col_half = lax.dynamic_slice(half_x, (jnp.int32(0), jnp.int32(0), (col_block * NTP * TILE).astype(jnp.int32)), (AUX, NOCC, NTP * TILE))
        products = jnp.einsum("ri,pik->prk", row_coef.astype(jnp.float32), col_half.astype(jnp.float32))
        tile_set = products.reshape(AUX, MT, TILE, NTP, TILE).transpose(1, 3, 0, 2, 4).reshape(MT * NTP, AUX, TILE, TILE)
        block_mask = lax.dynamic_slice(tile_mask, ((row_block * MT).astype(jnp.int32), (col_block * NTP).astype(jnp.int32)), (MT, NTP))
        block_owner = lax.dynamic_slice(tile_owner, ((row_block * MT).astype(jnp.int32), (col_block * NTP).astype(jnp.int32)), (MT, NTP))
        slot_tile, filled = route_slots(block_mask, block_owner, N_PAN)
        picked = jnp.take(tile_set, slot_tile.reshape(-1), axis=0).reshape(N_PAN, SCAP, AUX, TILE, TILE)
        return (picked * filled.astype(jnp.float32)[:, :, None, None, None]).astype(jnp.bfloat16)

    every = lax.map(one_block, jnp.arange(N_OCC * N_PAN, dtype=jnp.int32))
    every = every.reshape(N_OCC, N_PAN, N_PAN, SCAP, AUX, TILE, TILE)
    return every.transpose(0, 2, 1, 3, 4, 5, 6)
```

```python
import functools

import jax
import jax.numpy as jnp
from jax import lax
from jax.experimental import pallas as pl
from jax.experimental.pallas import tpu as pltpu
from jax.sharding import PartitionSpec as P

AUX = 2
TILE = 128
SCAP = 2
CHUNKS = 5
MESH = pl.DeviceIdType.MESH


def route_slots(block_mask, block_owner, owners):
    usable = block_mask.reshape(-1)
    owners_of = block_owner.reshape(-1)
    belongs = (
        (usable[:, None] == 1)
        & (owners_of[:, None] == jnp.arange(owners, dtype=jnp.int32)[None, :])
    ).astype(jnp.int32)
    order_rank = jnp.cumsum(belongs, axis=0) - belongs
    matched = belongs[:, :, None] * (
        order_rank[:, :, None] == jnp.arange(SCAP, dtype=jnp.int32)[None, None, :]
    ).astype(jnp.int32)
    tile_index = jnp.arange(usable.shape[0], dtype=jnp.int32)
    slot_tile = jnp.sum(matched * tile_index[:, None, None], axis=0)
    filled = jnp.sum(matched, axis=0)
    return (slot_tile, filled)


def block_slots(tile_mask, tile_owner, row_tiles, col_tiles, panels):
    row_block = lax.axis_index("occ")
    col_block = lax.axis_index("pan")
    corner = (row_block * row_tiles, col_block * col_tiles)
    block_mask = lax.dynamic_slice(tile_mask, corner, (row_tiles, col_tiles))
    block_owner = lax.dynamic_slice(tile_owner, corner, (row_tiles, col_tiles))
    return route_slots(block_mask, block_owner, panels)


def by_collectives(gamma_ia, coef_virt, coef_occ, tile_mask, tile_owner):
    panels = lax.axis_size("pan")
    occ_local = gamma_ia.shape[1]
    panel_width = coef_virt.shape[0] // panels
    row_tiles = coef_occ.shape[0] // TILE
    col_tiles = panel_width // TILE
    gamma_flat = gamma_ia.reshape(AUX * occ_local, gamma_ia.shape[2])
    summed = lax.psum_scatter(
        lax.dot_general(
            coef_virt, gamma_flat, (((1,), (1,)), ((), ())), preferred_element_type=jnp.float32
        ),
        "pan",
        scatter_dimension=0,
        tiled=True,
    )
    half_x = summed.astype(jnp.bfloat16).reshape(panel_width, AUX, occ_local)
    whole_x = lax.all_gather(half_x, "occ", axis=2, tiled=True)
    slot_tile, filled = block_slots(tile_mask, tile_owner, row_tiles, col_tiles, panels)
    flat_slots = slot_tile.reshape(-1)
    row_set = jnp.take(
        coef_occ.reshape(row_tiles, TILE, coef_occ.shape[1]), flat_slots // col_tiles, axis=0
    )
    col_set = jnp.take(
        whole_x.reshape(col_tiles, TILE, AUX, whole_x.shape[2]), flat_slots % col_tiles, axis=0
    )
    picked = jnp.einsum("sri,skpi->sprk", row_set, col_set, preferred_element_type=jnp.float32)
    picked = (
        picked.reshape(panels, SCAP, AUX, TILE, TILE)
        * filled.astype(jnp.float32)[:, :, None, None, None]
    )
    arrived = lax.all_to_all(
        picked.astype(jnp.bfloat16), "pan", split_axis=0, concat_axis=0, tiled=True
    )
    return arrived[None, None]


def kernel(
    n_occ, n_pan, chunks,
    rows_of, cols_of, filled_of, gamma_ref, virt_ref, occ_ref, out_ref,
    virt, coef, send_c, recv_c, keep_a, keep_b, send_a, recv_a, send_b, recv_b,
    keep_2, send_2a, recv_2a, send_2b, recv_2b, whole, picked,
    load_sem, coef_sem, own_sem,
    c_out, c_in, a_out, a_in, b_out, b_in, a2_out, a2_in, b2_out, b2_in,
    z_out, z_in, t_out, t_in,
):
    o = lax.axis_index("occ")
    s = lax.axis_index("pan")
    core = lax.rem(s, 2)
    x = lax.rem(s // 2, 2)
    y = s // 4
    other_core = s + 1 - 2 * core
    other_x = s + 2 - 4 * x
    other_y = s + 4 - 8 * y
    group = n_pan // 2
    width = virt.shape[3]
    tiles = width // TILE
    half = gamma_ref.shape[1]

    def load(q, cc):
        return pltpu.make_async_copy(
            virt_ref.at[:, cc, pl.ds(pl.multiple_of(q * width, width), width), :],
            virt.at[q, cc],
            load_sem.at[q, cc],
        )

    for q in range(chunks):
        load(q, 1 - core).start()
        load(q, core).start()
    fetch = pltpu.make_async_copy(occ_ref, coef, coef_sem)
    fetch.start()

    barrier = pltpu.get_barrier_semaphore()
    for d in range(1, n_pan):
        pl.semaphore_signal(
            barrier, inc=1, device_id=(o, lax.rem(s + d, n_pan)), device_id_type=MESH
        )
    for d in range(1, n_occ):
        pl.semaphore_signal(
            barrier, inc=1, device_id=(lax.rem(o + d, n_occ), s), device_id_type=MESH
        )
    pl.semaphore_wait(barrier, n_pan + n_occ - 2)

    def remote(src, dst, out_sem, in_sem, pan, row=None):
        return pltpu.make_async_remote_copy(
            src_ref=src, dst_ref=dst, send_sem=out_sem, recv_sem=in_sem,
            device_id=(o if row is None else row, pan), device_id_type=MESH,
        )

    def copy_c(q):
        return remote(send_c.at[q], recv_c.at[q], c_out.at[q], c_in.at[q], other_core)

    def copy_a(q):
        return remote(send_a.at[q], recv_a.at[q], a_out.at[q], a_in.at[q], other_x)

    def copy_b(q):
        return remote(send_b.at[q], recv_b.at[q], b_out.at[q], b_in.at[q], other_y)

    def copy_2a(q):
        return remote(send_2a.at[q], recv_2a.at[q], a2_out.at[q], a2_in.at[q], other_y)

    def copy_2b(q):
        return remote(send_2b.at[q], recv_2b.at[q], b2_out.at[q], b2_in.at[q], other_x)

    def copy_z(q, d, source):
        part = whole.at[source, pl.ds(q * tiles, tiles)]
        return remote(
            part, part, z_out.at[d - 1, q], z_in.at[d - 1, q], s, lax.rem(o + d, n_occ)
        )

    def product(q, cc, g):
        return lax.dot_general(
            virt[q, cc, g],
            gamma_ref[...].reshape(AUX * half, gamma_ref.shape[2]),
            (((1,), (1,)), ((), ())),
            preferred_element_type=jnp.float32,
        )

    def step(it, carry):
        @pl.when(it >= 3)
        def _():
            q = it - 3
            copy_2a(q).wait_recv()
            copy_2b(q).wait_recv()
            for p, arrived in ((0, recv_2a), (1, recv_2b)):
                total = keep_2[p] + arrived[q].astype(jnp.float32)
                total = total.astype(jnp.bfloat16)
                for t in range(tiles):
                    whole[o, q * tiles + t, p] = total[t * TILE:(t + 1) * TILE]
            for d in range(1, n_occ):
                copy_z(q, d, o).start()

        @pl.when((it >= 2) & (it < chunks + 2))
        def _():
            q = it - 2
            copy_a(q).wait_recv()
            send_2a[q] = (keep_a[1] + recv_a[q, 1].astype(jnp.float32)).astype(jnp.bfloat16)
            copy_2a(q).start()
            copy_b(q).wait_recv()
            send_2b[q] = (keep_b[1] + recv_b[q, 1].astype(jnp.float32)).astype(jnp.bfloat16)
            copy_2b(q).start()
            keep_2[0] = keep_a[0] + recv_a[q, 0].astype(jnp.float32)
            keep_2[1] = keep_b[0] + recv_b[q, 0].astype(jnp.float32)

        @pl.when((it >= 1) & (it < chunks + 1))
        def _():
            q = it - 1
            load(q, core).wait()
            copy_c(q).wait_recv()
            for b, a in ((1, 1), (0, 1), (1, 0), (0, 0)):
                gx = x + a - 2 * x * a
                gy = y + b - 2 * y * b
                g = gy * 2 + gx
                total = product(q, core, g) + recv_c[q, g].astype(jnp.float32)
                if a:
                    send_a[q, b] = total[:, :half].astype(jnp.bfloat16)
                else:
                    keep_a[b] = total[:, :half]
                if b:
                    send_b[q, a] = total[:, half:].astype(jnp.bfloat16)
                else:
                    keep_b[a] = total[:, half:]
                if (b, a) == (0, 1):
                    copy_a(q).start()
                if (b, a) == (1, 0):
                    copy_b(q).start()

        @pl.when(it < chunks)
        def _():
            load(it, 1 - core).wait()

            def one(g, c):
                send_c[it, g] = product(it, 1 - core, g).astype(jnp.bfloat16)
                return c

            lax.fori_loop(0, group, one, 0)
            copy_c(it).start()

        return carry

    lax.fori_loop(0, chunks + 3, step, 0)

    fetch.wait()
    for d in range(1, n_occ):
        def arrive(q, c, d=d):
            copy_z(q, d, lax.rem(o + n_occ - d, n_occ)).wait_recv()
            return c
        lax.fori_loop(0, chunks, arrive, 0)

    def tile_send(d):
        j = lax.rem(s + d, n_pan)
        return remote(
            picked.at[j], out_ref.at[s], t_out.at[d - 1], t_in.at[d - 1], j
        )

    def one_owner(d, c):
        j = lax.rem(s + d, n_pan)
        for k in range(SCAP):
            row = rows_of[j * SCAP + k]
            col = cols_of[j * SCAP + k]
            kept = filled_of[j * SCAP + k].astype(jnp.float32)
            total = jnp.zeros((TILE, AUX * TILE), jnp.float32)
            for z in range(n_occ):
                total += lax.dot_general(
                    coef[row, :, z * half:(z + 1) * half],
                    whole[z, col].reshape(AUX * TILE, half),
                    (((1,), (1,)), ((), ())),
                    preferred_element_type=jnp.float32,
                )
            total = (total * kept).astype(jnp.bfloat16)
            for p in range(AUX):
                picked[j, k, p] = total[:, p * TILE:(p + 1) * TILE]

        @pl.when(d < n_pan)
        def _():
            tile_send(d).start()

        return c

    lax.fori_loop(1, n_pan + 1, one_owner, 0)
    own = pltpu.make_async_copy(picked.at[s], out_ref.at[s], own_sem)
    own.start()

    def drain(q, c):
        for copy in (copy_c, copy_a, copy_b, copy_2a, copy_2b):
            copy(q).wait_send()
        for d in range(1, n_occ):
            copy_z(q, d, o).wait_send()
        return c

    lax.fori_loop(0, chunks, drain, 0)

    def finish(d, c):
        tile_send(d).wait_send()
        source = lax.rem(s + n_pan - d, n_pan)
        remote(
            picked.at[source], out_ref.at[source], t_out.at[d - 1], t_in.at[d - 1], source
        ).wait_recv()
        return c

    lax.fori_loop(1, n_pan, finish, 0)
    own.wait()


def by_kernel(n_occ, n_pan, gamma_ia, coef_virt, coef_occ, tile_mask, tile_owner):
    half = gamma_ia.shape[1]
    depth = gamma_ia.shape[2]
    panel_width = coef_virt.shape[0] // n_pan
    row_tiles = coef_occ.shape[0] // TILE
    col_tiles = panel_width // TILE
    chunks = CHUNKS if col_tiles % CHUNKS == 0 else 1
    width = panel_width // chunks
    group = n_pan // 2
    slot_tile, filled = block_slots(tile_mask, tile_owner, row_tiles, col_tiles, n_pan)
    flat_slots = slot_tile.reshape(-1)
    bf16, f32 = jnp.bfloat16, jnp.float32
    dma = pltpu.SemaphoreType.DMA
    smem = pl.BlockSpec(memory_space=pltpu.SMEM)
    hbm = pl.BlockSpec(memory_space=pl.ANY)
    arrived = pl.pallas_call(
        functools.partial(kernel, n_occ, n_pan, chunks),
        out_shape=jax.ShapeDtypeStruct((n_pan, SCAP, AUX, TILE, TILE), bf16),
        in_specs=[smem, smem, smem, pl.BlockSpec(memory_space=pltpu.VMEM), hbm, hbm],
        out_specs=hbm,
        scratch_shapes=[
            pltpu.VMEM((chunks, 2, group, width, depth), bf16),
            pltpu.VMEM((row_tiles, TILE, coef_occ.shape[1]), bf16),
            pltpu.VMEM((chunks, group, width, AUX * half), bf16),
            pltpu.VMEM((chunks, group, width, AUX * half), bf16),
            pltpu.VMEM((2, width, half), f32),
            pltpu.VMEM((2, width, half), f32),
            pltpu.VMEM((chunks, 2, width, half), bf16),
            pltpu.VMEM((chunks, 2, width, half), bf16),
            pltpu.VMEM((chunks, 2, width, half), bf16),
            pltpu.VMEM((chunks, 2, width, half), bf16),
            pltpu.VMEM((2, width, half), f32),
            pltpu.VMEM((chunks, width, half), bf16),
            pltpu.VMEM((chunks, width, half), bf16),
            pltpu.VMEM((chunks, width, half), bf16),
            pltpu.VMEM((chunks, width, half), bf16),
            pltpu.VMEM((n_occ, col_tiles, AUX, TILE, half), bf16),
            pltpu.VMEM((n_pan, SCAP, AUX, TILE, TILE), bf16),
            dma((chunks, 2)), dma, dma,
            *[dma((chunks,)) for _ in range(10)],
            dma((n_occ - 1, chunks)), dma((n_occ - 1, chunks)),
            dma((n_pan - 1,)), dma((n_pan - 1,)),
        ],
        compiler_params=pltpu.CompilerParams(
            collective_id=0, has_side_effects=True, vmem_limit_bytes=67043328
        ),
    )(
        flat_slots // col_tiles,
        flat_slots % col_tiles,
        filled.reshape(-1),
        gamma_ia,
        coef_virt.reshape(group, 2, panel_width, depth),
        coef_occ.reshape(row_tiles, TILE, coef_occ.shape[1]),
    )
    return arrived[None, None]


def solution(mesh):
    n_occ, n_pan = mesh.shape["occ"], mesh.shape["pan"]
    local = functools.partial(by_kernel, n_occ, n_pan) if n_pan == 8 else by_collectives
    return jax.shard_map(
        local,
        mesh=mesh,
        in_specs=(P(None, "occ", "pan"), P(None, "pan"), P("occ", None), P(), P()),
        out_specs=P("occ", "pan", None, None, None, None, None),
        check_vma=False,
    )
```

```python
import functools

import jax
import jax.numpy as jnp
from jax import lax
from jax.experimental import pallas as pl
from jax.experimental.pallas import tpu as pltpu
from jax.sharding import PartitionSpec as P

AUX = 2
TILE = 128
SCAP = 2
PARTS = 5
MESH = pl.DeviceIdType.MESH


def route_slots(block_mask, block_owner, owners):
    usable = block_mask.reshape(-1)
    owners_of = block_owner.reshape(-1)
    belongs = (
        (usable[:, None] == 1)
        & (owners_of[:, None] == jnp.arange(owners, dtype=jnp.int32)[None, :])
    ).astype(jnp.int32)
    order_rank = jnp.cumsum(belongs, axis=0) - belongs
    matched = belongs[:, :, None] * (
        order_rank[:, :, None] == jnp.arange(SCAP, dtype=jnp.int32)[None, None, :]
    ).astype(jnp.int32)
    tile_index = jnp.arange(usable.shape[0], dtype=jnp.int32)
    slot_tile = jnp.sum(matched * tile_index[:, None, None], axis=0)
    filled = jnp.sum(matched, axis=0)
    return (slot_tile, filled)


def block_slots(tile_mask, tile_owner, row_tiles, col_tiles, panels):
    row_block = lax.axis_index("occ")
    col_block = lax.axis_index("pan")
    corner = (row_block * row_tiles, col_block * col_tiles)
    block_mask = lax.dynamic_slice(tile_mask, corner, (row_tiles, col_tiles))
    block_owner = lax.dynamic_slice(tile_owner, corner, (row_tiles, col_tiles))
    return route_slots(block_mask, block_owner, panels)


def by_collectives(gamma_ia, coef_virt, coef_occ, tile_mask, tile_owner):
    panels = lax.axis_size("pan")
    occ_local = gamma_ia.shape[1]
    panel_width = coef_virt.shape[0] // panels
    row_tiles = coef_occ.shape[0] // TILE
    col_tiles = panel_width // TILE
    gamma_flat = gamma_ia.reshape(AUX * occ_local, gamma_ia.shape[2])
    summed = lax.psum_scatter(
        lax.dot_general(
            coef_virt, gamma_flat, (((1,), (1,)), ((), ())), preferred_element_type=jnp.float32
        ),
        "pan",
        scatter_dimension=0,
        tiled=True,
    )
    half_x = summed.astype(jnp.bfloat16).reshape(panel_width, AUX, occ_local)
    whole_x = lax.all_gather(half_x, "occ", axis=2, tiled=True)
    slot_tile, filled = block_slots(tile_mask, tile_owner, row_tiles, col_tiles, panels)
    flat_slots = slot_tile.reshape(-1)
    row_set = jnp.take(
        coef_occ.reshape(row_tiles, TILE, coef_occ.shape[1]), flat_slots // col_tiles, axis=0
    )
    col_set = jnp.take(
        whole_x.reshape(col_tiles, TILE, AUX, whole_x.shape[2]), flat_slots % col_tiles, axis=0
    )
    picked = jnp.einsum("sri,skpi->sprk", row_set, col_set, preferred_element_type=jnp.float32)
    picked = (
        picked.reshape(panels, SCAP, AUX, TILE, TILE)
        * filled.astype(jnp.float32)[:, :, None, None, None]
    )
    arrived = lax.all_to_all(
        picked.astype(jnp.bfloat16), "pan", split_axis=0, concat_axis=0, tiled=True
    )
    return arrived[None, None]


def kernel(
    n_occ, n_pan, parts,
    row_of, col_of, kept_of, gamma_ref, virt_ref, occ_ref, out_ref,
    gamma, virt, coef, send_c, recv_c, keep_a, keep_b, send_a, recv_a, send_b, recv_b,
    keep_2, send_2a, recv_2a, send_2b, recv_2b, whole_0, whole_1, picked,
    load_sem, coef_sem, own_sem,
    c_out, c_in, a_out, a_in, b_out, b_in, a2_out, a2_in, b2_out, b2_in,
    z_out, z_in, t_out, t_in,
):
    o = lax.axis_index("occ")
    s = lax.axis_index("pan")
    core = lax.rem(s, 2)
    x = lax.rem(s // 2, 2)
    y = s // 4
    other_core = s + 1 - 2 * core
    other_x = s + 2 - 4 * x
    other_y = s + 4 - 8 * y
    group = n_pan // 2
    width = virt.shape[3]
    tiles = width // TILE
    half = gamma.shape[1]
    quarter = half // 2
    chunks = AUX * parts
    wholes = (whole_0, whole_1)

    def load(q, pan):
        first = pl.multiple_of(pan * (parts * width) + q * width, width)
        return pltpu.make_async_copy(
            virt_ref.at[:, pl.ds(first, width)], virt.at[q, pan], load_sem.at[q, pan]
        )

    for q in range(parts):
        for g in range(group):
            load(q, 2 * g + 1 - core).start()
        for g in range(group):
            load(q, 2 * g + core).start()
    fetch = pltpu.make_async_copy(occ_ref, coef, coef_sem)
    fetch.start()

    barrier = pltpu.get_barrier_semaphore()
    for d in range(1, n_pan):
        pl.semaphore_signal(
            barrier, inc=1, device_id=(o, lax.rem(s + d, n_pan)), device_id_type=MESH
        )
    for d in range(1, n_occ):
        pl.semaphore_signal(
            barrier, inc=1, device_id=(lax.rem(o + d, n_occ), s), device_id_type=MESH
        )
    for p in range(AUX):
        gamma[p] = gamma_ref[p].T
    pl.semaphore_wait(barrier, n_pan + n_occ - 2)

    def remote(src, dst, out_sem, in_sem, pan, row=None):
        return pltpu.make_async_remote_copy(
            src_ref=src, dst_ref=dst, send_sem=out_sem, recv_sem=in_sem,
            device_id=(o if row is None else row, pan), device_id_type=MESH,
        )

    def copy_c(q):
        return remote(send_c.at[q], recv_c.at[q], c_out.at[q], c_in.at[q], other_core)

    def copy_a(q):
        return remote(send_a.at[q], recv_a.at[q], a_out.at[q], a_in.at[q], other_x)

    def copy_b(q):
        return remote(send_b.at[q], recv_b.at[q], b_out.at[q], b_in.at[q], other_y)

    def copy_2a(q):
        return remote(send_2a.at[q], recv_2a.at[q], a2_out.at[q], a2_in.at[q], other_y)

    def copy_2b(q):
        return remote(send_2b.at[q], recv_2b.at[q], b2_out.at[q], b2_in.at[q], other_x)

    def copy_z(p, q, d, source):
        part = wholes[p].at[source, pl.ds(q * tiles, tiles)]
        return remote(
            part, part, z_out.at[d - 1, p, q], z_in.at[d - 1, p, q], s, lax.rem(o + d, n_occ)
        )

    def product(p, q, pan):
        return lax.dot_general(
            gamma[p],
            virt[q, pan],
            (((1,), (0,)), ((), ())),
            preferred_element_type=jnp.float32,
        )

    def step(it, carry):
        for p in range(AUX):
            @pl.when((it >= 3 + p * parts) & (it < 3 + (p + 1) * parts))
            def _(p=p):
                ch = it - 3
                q = ch - p * parts
                copy_2a(ch).wait_recv()
                copy_2b(ch).wait_recv()
                for h, arrived in ((0, recv_2a), (1, recv_2b)):
                    total = keep_2[h] + arrived[ch].astype(jnp.float32)
                    total = total.astype(jnp.bfloat16)
                    for t in range(tiles):
                        wholes[p][o, q * tiles + t, h * quarter:(h + 1) * quarter] = total[
                            :, t * TILE:(t + 1) * TILE
                        ]
                for d in range(1, n_occ):
                    copy_z(p, q, d, o).start()

        @pl.when((it >= 2) & (it < chunks + 2))
        def _():
            q = it - 2
            copy_a(q).wait_recv()
            send_2a[q] = (keep_a[1] + recv_a[q, 1].astype(jnp.float32)).astype(jnp.bfloat16)
            copy_2a(q).start()
            copy_b(q).wait_recv()
            send_2b[q] = (keep_b[1] + recv_b[q, 1].astype(jnp.float32)).astype(jnp.bfloat16)
            copy_2b(q).start()
            keep_2[0] = keep_a[0] + recv_a[q, 0].astype(jnp.float32)
            keep_2[1] = keep_b[0] + recv_b[q, 0].astype(jnp.float32)

        for p in range(AUX):
            @pl.when((it >= 1 + p * parts) & (it < 1 + (p + 1) * parts))
            def _(p=p):
                ch = it - 1
                q = ch - p * parts
                if p == 0:
                    for g in range(group):
                        load(q, 2 * g + core).wait()
                copy_c(ch).wait_recv()
                for b, a in ((1, 1), (0, 1), (1, 0), (0, 0)):
                    gx = x + a - 2 * x * a
                    gy = y + b - 2 * y * b
                    g = gy * 2 + gx
                    total = product(p, q, 2 * g + core) + recv_c[ch, g].astype(jnp.float32)
                    if a:
                        send_a[ch, b] = total[:quarter].astype(jnp.bfloat16)
                    else:
                        keep_a[b] = total[:quarter]
                    if b:
                        send_b[ch, a] = total[quarter:].astype(jnp.bfloat16)
                    else:
                        keep_b[a] = total[quarter:]
                    if (b, a) == (0, 1):
                        copy_a(ch).start()
                    if (b, a) == (1, 0):
                        copy_b(ch).start()

        for p in range(AUX):
            @pl.when((it >= p * parts) & (it < (p + 1) * parts))
            def _(p=p):
                q = it - p * parts
                if p == 0:
                    for g in range(group):
                        load(q, 2 * g + 1 - core).wait()

                def one(g, c):
                    send_c[it, g] = product(p, q, 2 * g + 1 - core).astype(jnp.bfloat16)
                    return c

                lax.fori_loop(0, group, one, 0)
                copy_c(it).start()

        return carry

    lax.fori_loop(0, chunks + 3, step, 0)

    fetch.wait()

    def tile_send(p, d, source, target):
        return remote(
            picked.at[p, target], out_ref.at[source, p],
            t_out.at[p, d - 1], t_in.at[p, d - 1], target,
        )

    def own(p):
        return pltpu.make_async_copy(picked.at[p, s], out_ref.at[s, p], own_sem.at[p])

    for p in range(AUX):
        for d in range(1, n_occ):
            def arrive(q, c, d=d):
                copy_z(p, q, d, lax.rem(o + n_occ - d, n_occ)).wait_recv()
                return c
            lax.fori_loop(0, parts, arrive, 0)

        def one_owner(d, c):
            j = lax.rem(s + d, n_pan)
            for k in range(SCAP):
                row = row_of[j * SCAP + k]
                col = col_of[j * SCAP + k]
                kept = kept_of[j * SCAP + k].astype(jnp.float32)
                total = lax.dot_general(
                    coef[row],
                    jnp.concatenate(
                        [wholes[p][z, col] for z in range(n_occ)]
                    ),
                    (((1,), (0,)), ((), ())),
                    preferred_element_type=jnp.float32,
                )
                picked[p, j, k] = (total * kept).astype(jnp.bfloat16)

            @pl.when(d < n_pan)
            def _():
                tile_send(p, d, s, j).start()

            return c

        lax.fori_loop(1, n_pan + 1, one_owner, 0)
        own(p).start()

    def drain(ch, c):
        for copy in (copy_c, copy_a, copy_b, copy_2a, copy_2b):
            copy(ch).wait_send()
        return c

    lax.fori_loop(0, chunks, drain, 0)

    for p in range(AUX):
        def drain_z(q, c):
            for d in range(1, n_occ):
                copy_z(p, q, d, o).wait_send()
            return c

        lax.fori_loop(0, parts, drain_z, 0)

        def finish(d, c):
            tile_send(p, d, s, lax.rem(s + d, n_pan)).wait_send()
            source = lax.rem(s + n_pan - d, n_pan)
            tile_send(p, d, source, source).wait_recv()
            return c

        lax.fori_loop(1, n_pan, finish, 0)
        own(p).wait()


def by_kernel(n_occ, n_pan, gamma_ia, coef_virt, coef_occ, tile_mask, tile_owner):
    half = gamma_ia.shape[1]
    depth = gamma_ia.shape[2]
    panel_width = coef_virt.shape[0] // n_pan
    row_tiles = coef_occ.shape[0] // TILE
    col_tiles = panel_width // TILE
    parts = PARTS if col_tiles % PARTS == 0 else 1
    width = panel_width // parts
    chunks = AUX * parts
    group = n_pan // 2
    quarter = half // 2
    slot_tile, filled = block_slots(tile_mask, tile_owner, row_tiles, col_tiles, n_pan)
    flat_slots = slot_tile.reshape(-1)
    bf16, f32 = jnp.bfloat16, jnp.float32
    dma = pltpu.SemaphoreType.DMA
    smem = pl.BlockSpec(memory_space=pltpu.SMEM)
    hbm = pl.BlockSpec(memory_space=pl.ANY)
    arrived = pl.pallas_call(
        functools.partial(kernel, n_occ, n_pan, parts),
        out_shape=jax.ShapeDtypeStruct((n_pan, AUX, SCAP, TILE, TILE), bf16),
        in_specs=[smem, smem, smem, pl.BlockSpec(memory_space=pltpu.VMEM), hbm, hbm],
        out_specs=hbm,
        scratch_shapes=[
            pltpu.VMEM((AUX, half, depth), bf16),
            pltpu.VMEM((parts, n_pan, depth, width), bf16),
            pltpu.VMEM((row_tiles, TILE, coef_occ.shape[1]), bf16),
            pltpu.VMEM((chunks, group, half, width), bf16),
            pltpu.VMEM((chunks, group, half, width), bf16),
            pltpu.VMEM((2, quarter, width), f32),
            pltpu.VMEM((2, quarter, width), f32),
            pltpu.VMEM((chunks, 2, quarter, width), bf16),
            pltpu.VMEM((chunks, 2, quarter, width), bf16),
            pltpu.VMEM((chunks, 2, quarter, width), bf16),
            pltpu.VMEM((chunks, 2, quarter, width), bf16),
            pltpu.VMEM((2, quarter, width), f32),
            pltpu.VMEM((chunks, quarter, width), bf16),
            pltpu.VMEM((chunks, quarter, width), bf16),
            pltpu.VMEM((chunks, quarter, width), bf16),
            pltpu.VMEM((chunks, quarter, width), bf16),
            pltpu.VMEM((n_occ, col_tiles, half, TILE), bf16),
            pltpu.VMEM((n_occ, col_tiles, half, TILE), bf16),
            pltpu.VMEM((AUX, n_pan, SCAP, TILE, TILE), bf16),
            dma((parts, n_pan)), dma, dma((AUX,)),
            *[dma((chunks,)) for _ in range(10)],
            dma((n_occ - 1, AUX, parts)), dma((n_occ - 1, AUX, parts)),
            dma((AUX, n_pan - 1)), dma((AUX, n_pan - 1)),
        ],
        compiler_params=pltpu.CompilerParams(
            collective_id=0, has_side_effects=True, vmem_limit_bytes=67043328
        ),
    )(
        flat_slots // col_tiles,
        flat_slots % col_tiles,
        filled.reshape(-1),
        jnp.swapaxes(gamma_ia, 1, 2),
        coef_virt.T,
        coef_occ.reshape(row_tiles, TILE, coef_occ.shape[1]),
    )
    return jnp.swapaxes(arrived, 1, 2)[None, None]


def solution(mesh):
    n_occ, n_pan = mesh.shape["occ"], mesh.shape["pan"]
    local = functools.partial(by_kernel, n_occ, n_pan) if n_pan == 8 else by_collectives
    return jax.shard_map(
        local,
        mesh=mesh,
        in_specs=(P(None, "occ", "pan"), P(None, "pan"), P("occ", None), P(), P()),
        out_specs=P("occ", "pan", None, None, None, None, None),
        check_vma=False,
    )
```

```python
import functools

import jax
import jax.numpy as jnp
from jax import lax
from jax.experimental import pallas as pl
from jax.experimental.pallas import tpu as pltpu
from jax.sharding import PartitionSpec as P

AUX = 2
TILE = 128
SCAP = 2
PARTS = 5
MESH = pl.DeviceIdType.MESH


def route_slots(block_mask, block_owner, owners):
    usable = block_mask.reshape(-1)
    owners_of = block_owner.reshape(-1)
    belongs = (
        (usable[:, None] == 1)
        & (owners_of[:, None] == jnp.arange(owners, dtype=jnp.int32)[None, :])
    ).astype(jnp.int32)
    order_rank = jnp.cumsum(belongs, axis=0) - belongs
    matched = belongs[:, :, None] * (
        order_rank[:, :, None] == jnp.arange(SCAP, dtype=jnp.int32)[None, None, :]
    ).astype(jnp.int32)
    tile_index = jnp.arange(usable.shape[0], dtype=jnp.int32)
    slot_tile = jnp.sum(matched * tile_index[:, None, None], axis=0)
    filled = jnp.sum(matched, axis=0)
    return (slot_tile, filled)


def block_slots(tile_mask, tile_owner, row_tiles, col_tiles, panels):
    row_block = lax.axis_index("occ")
    col_block = lax.axis_index("pan")
    corner = (row_block * row_tiles, col_block * col_tiles)
    block_mask = lax.dynamic_slice(tile_mask, corner, (row_tiles, col_tiles))
    block_owner = lax.dynamic_slice(tile_owner, corner, (row_tiles, col_tiles))
    return route_slots(block_mask, block_owner, panels)


def by_collectives(gamma_ia, coef_virt, coef_occ, tile_mask, tile_owner):
    panels = lax.axis_size("pan")
    occ_local = gamma_ia.shape[1]
    panel_width = coef_virt.shape[0] // panels
    row_tiles = coef_occ.shape[0] // TILE
    col_tiles = panel_width // TILE
    gamma_flat = gamma_ia.reshape(AUX * occ_local, gamma_ia.shape[2])
    summed = lax.psum_scatter(
        lax.dot_general(
            coef_virt, gamma_flat, (((1,), (1,)), ((), ())), preferred_element_type=jnp.float32
        ),
        "pan",
        scatter_dimension=0,
        tiled=True,
    )
    half_x = summed.astype(jnp.bfloat16).reshape(panel_width, AUX, occ_local)
    whole_x = lax.all_gather(half_x, "occ", axis=2, tiled=True)
    slot_tile, filled = block_slots(tile_mask, tile_owner, row_tiles, col_tiles, panels)
    flat_slots = slot_tile.reshape(-1)
    row_set = jnp.take(
        coef_occ.reshape(row_tiles, TILE, coef_occ.shape[1]), flat_slots // col_tiles, axis=0
    )
    col_set = jnp.take(
        whole_x.reshape(col_tiles, TILE, AUX, whole_x.shape[2]), flat_slots % col_tiles, axis=0
    )
    picked = jnp.einsum("sri,skpi->sprk", row_set, col_set, preferred_element_type=jnp.float32)
    picked = (
        picked.reshape(panels, SCAP, AUX, TILE, TILE)
        * filled.astype(jnp.float32)[:, :, None, None, None]
    )
    arrived = lax.all_to_all(
        picked.astype(jnp.bfloat16), "pan", split_axis=0, concat_axis=0, tiled=True
    )
    return arrived[None, None]


def kernel(
    n_occ, n_pan, parts,
    row_of, col_of, kept_of, gamma_ref, virt_ref, occ_ref, out_ref,
    gamma, virt, coef, send_c, recv_c, keep_a, keep_b, send_a, recv_a, send_b, recv_b,
    keep_2, send_2a, recv_2a, send_2b, recv_2b, whole_0, whole_1, picked,
    load_sem, coef_sem, own_sem,
    c_out, c_in, a_out, a_in, b_out, b_in, a2_out, a2_in, b2_out, b2_in,
    z_out, z_in, t_out, t_in,
):
    o = lax.axis_index("occ")
    s = lax.axis_index("pan")
    core = lax.rem(s, 2)
    x = lax.rem(s // 2, 2)
    y = s // 4
    other_core = s + 1 - 2 * core
    other_x = s + 2 - 4 * x
    other_y = s + 4 - 8 * y
    group = n_pan // 2
    width = virt.shape[3]
    tiles = width // TILE
    half = gamma.shape[1]
    quarter = half // 2
    chunks = AUX * parts
    wholes = (whole_0, whole_1)

    def load(q, pan):
        first = pl.multiple_of(pan * (parts * width) + q * width, width)
        return pltpu.make_async_copy(
            virt_ref.at[:, pl.ds(first, width)], virt.at[q, pan], load_sem.at[q, pan]
        )

    for q in range(parts):
        for g in range(group):
            load(q, 2 * g + 1 - core).start()
        for g in range(group):
            load(q, 2 * g + core).start()
    fetch = pltpu.make_async_copy(occ_ref, coef, coef_sem)
    fetch.start()

    barrier = pltpu.get_barrier_semaphore()
    for d in range(1, n_pan):
        pl.semaphore_signal(
            barrier, inc=1, device_id=(o, lax.rem(s + d, n_pan)), device_id_type=MESH
        )
    for d in range(1, n_occ):
        pl.semaphore_signal(
            barrier, inc=1, device_id=(lax.rem(o + d, n_occ), s), device_id_type=MESH
        )
    for p in range(AUX):
        gamma[p] = gamma_ref[p].T
    pl.semaphore_wait(barrier, n_pan + n_occ - 2)

    def remote(src, dst, out_sem, in_sem, pan, row=None):
        return pltpu.make_async_remote_copy(
            src_ref=src, dst_ref=dst, send_sem=out_sem, recv_sem=in_sem,
            device_id=(o if row is None else row, pan), device_id_type=MESH,
        )

    def copy_c(q):
        return remote(send_c.at[q], recv_c.at[q], c_out.at[q], c_in.at[q], other_core)

    def copy_a(q):
        return remote(send_a.at[q], recv_a.at[q], a_out.at[q], a_in.at[q], other_x)

    def copy_b(q):
        return remote(send_b.at[q], recv_b.at[q], b_out.at[q], b_in.at[q], other_y)

    def copy_2a(q):
        return remote(send_2a.at[q], recv_2a.at[q], a2_out.at[q], a2_in.at[q], other_y)

    def copy_2b(q):
        return remote(send_2b.at[q], recv_2b.at[q], b2_out.at[q], b2_in.at[q], other_x)

    last = n_occ - 1

    def copy_z(p, q, way, hop, source):
        part = wholes[p].at[source, pl.ds(q * tiles, tiles)]
        target = jnp.clip(o + 1 - 2 * way, 0, last)
        return remote(
            part, part, z_out.at[way, hop, p, q], z_in.at[way, hop, p, q], s, target
        )

    def sends(way, hop):
        return (o < last) & (o >= hop) if way == 0 else (o > 0) & (o + hop <= last)

    def held(way, hop):
        return o - hop if way == 0 else o + hop

    def product(p, q, pan):
        return lax.dot_general(
            gamma[p],
            virt[q, pan],
            (((1,), (0,)), ((), ())),
            preferred_element_type=jnp.float32,
        )

    def step(it, carry):
        for p in range(AUX):
            @pl.when((it >= 3 + p * parts) & (it < 3 + (p + 1) * parts))
            def _(p=p):
                ch = it - 3
                q = ch - p * parts
                copy_2a(ch).wait_recv()
                copy_2b(ch).wait_recv()
                for h, arrived in ((0, recv_2a), (1, recv_2b)):
                    total = keep_2[h] + arrived[ch].astype(jnp.float32)
                    total = total.astype(jnp.bfloat16)
                    for t in range(tiles):
                        wholes[p][o, q * tiles + t, h * quarter:(h + 1) * quarter] = total[
                            :, t * TILE:(t + 1) * TILE
                        ]

            for way in range(2):
                @pl.when(
                    (it >= 3 + p * parts) & (it < 3 + (p + 1) * parts) & sends(way, 0)
                )
                def _(p=p, way=way):
                    copy_z(p, it - 3 - p * parts, way, 0, o).start()

        @pl.when((it >= 2) & (it < chunks + 2))
        def _():
            q = it - 2
            copy_a(q).wait_recv()
            send_2a[q] = (keep_a[1] + recv_a[q, 1].astype(jnp.float32)).astype(jnp.bfloat16)
            copy_2a(q).start()
            copy_b(q).wait_recv()
            send_2b[q] = (keep_b[1] + recv_b[q, 1].astype(jnp.float32)).astype(jnp.bfloat16)
            copy_2b(q).start()
            keep_2[0] = keep_a[0] + recv_a[q, 0].astype(jnp.float32)
            keep_2[1] = keep_b[0] + recv_b[q, 0].astype(jnp.float32)

        for p in range(AUX):
            @pl.when((it >= 1 + p * parts) & (it < 1 + (p + 1) * parts))
            def _(p=p):
                ch = it - 1
                q = ch - p * parts
                if p == 0:
                    for g in range(group):
                        load(q, 2 * g + core).wait()
                copy_c(ch).wait_recv()
                for b, a in ((1, 1), (0, 1), (1, 0), (0, 0)):
                    gx = x + a - 2 * x * a
                    gy = y + b - 2 * y * b
                    g = gy * 2 + gx
                    total = product(p, q, 2 * g + core) + recv_c[ch, g].astype(jnp.float32)
                    if a:
                        send_a[ch, b] = total[:quarter].astype(jnp.bfloat16)
                    else:
                        keep_a[b] = total[:quarter]
                    if b:
                        send_b[ch, a] = total[quarter:].astype(jnp.bfloat16)
                    else:
                        keep_b[a] = total[quarter:]
                    if (b, a) == (0, 1):
                        copy_a(ch).start()
                    if (b, a) == (1, 0):
                        copy_b(ch).start()

        for p in range(AUX):
            @pl.when((it >= p * parts) & (it < (p + 1) * parts))
            def _(p=p):
                q = it - p * parts
                if p == 0:
                    for g in range(group):
                        load(q, 2 * g + 1 - core).wait()

                def one(g, c):
                    send_c[it, g] = product(p, q, 2 * g + 1 - core).astype(jnp.bfloat16)
                    return c

                lax.fori_loop(0, group, one, 0)
                copy_c(it).start()

        for hop in range(1, last):
            lag = 3 + 2 * hop
            for p in range(AUX):
                for way in range(2):
                    @pl.when(
                        (it >= lag + p * parts)
                        & (it < lag + (p + 1) * parts)
                        & sends(way, hop)
                    )
                    def _(p=p, way=way, hop=hop, lag=lag):
                        q = it - lag - p * parts
                        copy_z(p, q, way, hop - 1, held(way, hop)).wait_recv()
                        copy_z(p, q, way, hop, held(way, hop)).start()

        return carry

    lax.fori_loop(0, chunks + 3 + 2 * max(last - 1, 0), step, 0)

    fetch.wait()

    def tile_send(p, d, source, target):
        return remote(
            picked.at[p, target], out_ref.at[source, p],
            t_out.at[p, d - 1], t_in.at[p, d - 1], target,
        )

    def own(p):
        return pltpu.make_async_copy(picked.at[p, s], out_ref.at[s, p], own_sem.at[p])

    for p in range(AUX):
        for hop in range(1, n_occ):
            for way, end in ((0, last), (1, 0)):
                @pl.when(o == end)
                def _(p=p, hop=hop, way=way):
                    def arrive(q, c):
                        copy_z(p, q, way, hop - 1, held(way, hop)).wait_recv()
                        return c

                    lax.fori_loop(0, parts, arrive, 0)

        def one_owner(d, c):
            j = lax.rem(s + d, n_pan)
            for k in range(SCAP):
                row = row_of[j * SCAP + k]
                col = col_of[j * SCAP + k]
                kept = kept_of[j * SCAP + k].astype(jnp.float32)
                total = lax.dot_general(
                    coef[row],
                    jnp.concatenate(
                        [wholes[p][z, col] for z in range(n_occ)]
                    ),
                    (((1,), (0,)), ((), ())),
                    preferred_element_type=jnp.float32,
                )
                picked[p, j, k] = (total * kept).astype(jnp.bfloat16)

            @pl.when(d < n_pan)
            def _():
                tile_send(p, d, s, j).start()

            return c

        lax.fori_loop(1, n_pan + 1, one_owner, 0)
        own(p).start()

    def drain(ch, c):
        for copy in (copy_c, copy_a, copy_b, copy_2a, copy_2b):
            copy(ch).wait_send()
        return c

    lax.fori_loop(0, chunks, drain, 0)

    for p in range(AUX):
        for hop in range(last):
            for way in range(2):
                @pl.when(sends(way, hop))
                def _(p=p, hop=hop, way=way):
                    def drain_z(q, c):
                        copy_z(p, q, way, hop, held(way, hop)).wait_send()
                        return c

                    lax.fori_loop(0, parts, drain_z, 0)

        def finish(d, c):
            tile_send(p, d, s, lax.rem(s + d, n_pan)).wait_send()
            source = lax.rem(s + n_pan - d, n_pan)
            tile_send(p, d, source, source).wait_recv()
            return c

        lax.fori_loop(1, n_pan, finish, 0)
        own(p).wait()


def by_kernel(n_occ, n_pan, gamma_ia, coef_virt, coef_occ, tile_mask, tile_owner):
    half = gamma_ia.shape[1]
    depth = gamma_ia.shape[2]
    panel_width = coef_virt.shape[0] // n_pan
    row_tiles = coef_occ.shape[0] // TILE
    col_tiles = panel_width // TILE
    parts = PARTS if col_tiles % PARTS == 0 else 1
    width = panel_width // parts
    chunks = AUX * parts
    group = n_pan // 2
    quarter = half // 2
    slot_tile, filled = block_slots(tile_mask, tile_owner, row_tiles, col_tiles, n_pan)
    flat_slots = slot_tile.reshape(-1)
    bf16, f32 = jnp.bfloat16, jnp.float32
    dma = pltpu.SemaphoreType.DMA
    smem = pl.BlockSpec(memory_space=pltpu.SMEM)
    hbm = pl.BlockSpec(memory_space=pl.ANY)
    arrived = pl.pallas_call(
        functools.partial(kernel, n_occ, n_pan, parts),
        out_shape=jax.ShapeDtypeStruct((n_pan, AUX, SCAP, TILE, TILE), bf16),
        in_specs=[smem, smem, smem, pl.BlockSpec(memory_space=pltpu.VMEM), hbm, hbm],
        out_specs=hbm,
        scratch_shapes=[
            pltpu.VMEM((AUX, half, depth), bf16),
            pltpu.VMEM((parts, n_pan, depth, width), bf16),
            pltpu.VMEM((row_tiles, TILE, coef_occ.shape[1]), bf16),
            pltpu.VMEM((chunks, group, half, width), bf16),
            pltpu.VMEM((chunks, group, half, width), bf16),
            pltpu.VMEM((2, quarter, width), f32),
            pltpu.VMEM((2, quarter, width), f32),
            pltpu.VMEM((chunks, 2, quarter, width), bf16),
            pltpu.VMEM((chunks, 2, quarter, width), bf16),
            pltpu.VMEM((chunks, 2, quarter, width), bf16),
            pltpu.VMEM((chunks, 2, quarter, width), bf16),
            pltpu.VMEM((2, quarter, width), f32),
            pltpu.VMEM((chunks, quarter, width), bf16),
            pltpu.VMEM((chunks, quarter, width), bf16),
            pltpu.VMEM((chunks, quarter, width), bf16),
            pltpu.VMEM((chunks, quarter, width), bf16),
            pltpu.VMEM((n_occ, col_tiles, half, TILE), bf16),
            pltpu.VMEM((n_occ, col_tiles, half, TILE), bf16),
            pltpu.VMEM((AUX, n_pan, SCAP, TILE, TILE), bf16),
            dma((parts, n_pan)), dma, dma((AUX,)),
            *[dma((chunks,)) for _ in range(10)],
            dma((2, n_occ - 1, AUX, parts)), dma((2, n_occ - 1, AUX, parts)),
            dma((AUX, n_pan - 1)), dma((AUX, n_pan - 1)),
        ],
        compiler_params=pltpu.CompilerParams(
            collective_id=0, has_side_effects=True, vmem_limit_bytes=67043328
        ),
    )(
        flat_slots // col_tiles,
        flat_slots % col_tiles,
        filled.reshape(-1),
        jnp.swapaxes(gamma_ia, 1, 2),
        coef_virt.T,
        coef_occ.reshape(row_tiles, TILE, coef_occ.shape[1]),
    )
    return jnp.swapaxes(arrived, 1, 2)[None, None]


def solution(mesh):
    n_occ, n_pan = mesh.shape["occ"], mesh.shape["pan"]
    local = functools.partial(by_kernel, n_occ, n_pan) if n_pan == 8 else by_collectives
    return jax.shard_map(
        local,
        mesh=mesh,
        in_specs=(P(None, "occ", "pan"), P(None, "pan"), P("occ", None), P(), P()),
        out_specs=P("occ", "pan", None, None, None, None, None),
        check_vma=False,
    )
```

```python
import functools

import jax
import jax.numpy as jnp
from jax import lax
from jax.experimental import pallas as pl
from jax.experimental.pallas import tpu as pltpu
from jax.sharding import PartitionSpec as P

AUX = 2
TILE = 128
SCAP = 2
PARTS = 5
MESH = pl.DeviceIdType.MESH


def route_slots(block_mask, block_owner, owners):
    usable = block_mask.reshape(-1)
    owners_of = block_owner.reshape(-1)
    belongs = (
        (usable[:, None] == 1)
        & (owners_of[:, None] == jnp.arange(owners, dtype=jnp.int32)[None, :])
    ).astype(jnp.int32)
    order_rank = jnp.cumsum(belongs, axis=0) - belongs
    matched = belongs[:, :, None] * (
        order_rank[:, :, None] == jnp.arange(SCAP, dtype=jnp.int32)[None, None, :]
    ).astype(jnp.int32)
    tile_index = jnp.arange(usable.shape[0], dtype=jnp.int32)
    slot_tile = jnp.sum(matched * tile_index[:, None, None], axis=0)
    filled = jnp.sum(matched, axis=0)
    return (slot_tile, filled)


def block_slots(tile_mask, tile_owner, row_tiles, col_tiles, panels):
    row_block = lax.axis_index("occ")
    col_block = lax.axis_index("pan")
    corner = (row_block * row_tiles, col_block * col_tiles)
    block_mask = lax.dynamic_slice(tile_mask, corner, (row_tiles, col_tiles))
    block_owner = lax.dynamic_slice(tile_owner, corner, (row_tiles, col_tiles))
    return route_slots(block_mask, block_owner, panels)


def by_collectives(gamma_ia, coef_virt, coef_occ, tile_mask, tile_owner):
    panels = lax.axis_size("pan")
    occ_local = gamma_ia.shape[1]
    panel_width = coef_virt.shape[0] // panels
    row_tiles = coef_occ.shape[0] // TILE
    col_tiles = panel_width // TILE
    gamma_flat = gamma_ia.reshape(AUX * occ_local, gamma_ia.shape[2])
    summed = lax.psum_scatter(
        lax.dot_general(
            coef_virt, gamma_flat, (((1,), (1,)), ((), ())), preferred_element_type=jnp.float32
        ),
        "pan",
        scatter_dimension=0,
        tiled=True,
    )
    half_x = summed.astype(jnp.bfloat16).reshape(panel_width, AUX, occ_local)
    whole_x = lax.all_gather(half_x, "occ", axis=2, tiled=True)
    slot_tile, filled = block_slots(tile_mask, tile_owner, row_tiles, col_tiles, panels)
    flat_slots = slot_tile.reshape(-1)
    row_set = jnp.take(
        coef_occ.reshape(row_tiles, TILE, coef_occ.shape[1]), flat_slots // col_tiles, axis=0
    )
    col_set = jnp.take(
        whole_x.reshape(col_tiles, TILE, AUX, whole_x.shape[2]), flat_slots % col_tiles, axis=0
    )
    picked = jnp.einsum("sri,skpi->sprk", row_set, col_set, preferred_element_type=jnp.float32)
    picked = (
        picked.reshape(panels, SCAP, AUX, TILE, TILE)
        * filled.astype(jnp.float32)[:, :, None, None, None]
    )
    arrived = lax.all_to_all(
        picked.astype(jnp.bfloat16), "pan", split_axis=0, concat_axis=0, tiled=True
    )
    return arrived[None, None]


def kernel(
    n_occ, n_pan, parts,
    row_of, col_of, kept_of, gamma_ref, virt_ref, occ_ref, out_ref,
    gamma, virt, coef, send_c, recv_c, keep_a, keep_b, send_a, recv_a, send_b, recv_b,
    keep_2, send_2a, recv_2a, send_2b, recv_2b, whole_0, whole_1, picked,
    load_sem, coef_sem, own_sem,
    c_out, c_in, a_out, a_in, b_out, b_in, a2_out, a2_in, b2_out, b2_in,
    z_out, z_in, t_out, t_in,
):
    o = lax.axis_index("occ")
    s = lax.axis_index("pan")
    core = lax.rem(s, 2)
    x = lax.rem(s // 2, 2)
    y = s // 4
    other_core = s + 1 - 2 * core
    other_x = s + 2 - 4 * x
    other_y = s + 4 - 8 * y
    group = n_pan // 2
    width = virt.shape[3]
    tiles = width // TILE
    half = gamma.shape[1]
    quarter = half // 2
    chunks = AUX * parts
    wholes = (whole_0, whole_1)

    def load(q, pan):
        first = pl.multiple_of(pan * (parts * width) + q * width, width)
        return pltpu.make_async_copy(
            virt_ref.at[:, pl.ds(first, width)], virt.at[q, pan], load_sem.at[q, pan]
        )

    def load_part(q):
        for g in range(group):
            load(q, 2 * g + 1 - core).start()
        for g in range(group):
            load(q, 2 * g + core).start()

    load_part(0)
    fetch = pltpu.make_async_copy(occ_ref, coef, coef_sem)

    barrier = pltpu.get_barrier_semaphore()
    for d in range(1, n_pan):
        pl.semaphore_signal(
            barrier, inc=1, device_id=(o, lax.rem(s + d, n_pan)), device_id_type=MESH
        )
    for d in range(1, n_occ):
        pl.semaphore_signal(
            barrier, inc=1, device_id=(lax.rem(o + d, n_occ), s), device_id_type=MESH
        )
    for p in range(AUX):
        gamma[p] = gamma_ref[p].T
    pl.semaphore_wait(barrier, n_pan + n_occ - 2)

    def remote(src, dst, out_sem, in_sem, pan, row=None):
        return pltpu.make_async_remote_copy(
            src_ref=src, dst_ref=dst, send_sem=out_sem, recv_sem=in_sem,
            device_id=(o if row is None else row, pan), device_id_type=MESH,
        )

    def copy_c(q):
        return remote(send_c.at[q], recv_c.at[q], c_out.at[q], c_in.at[q], other_core)

    def copy_a(q):
        return remote(send_a.at[q], recv_a.at[q], a_out.at[q], a_in.at[q], other_x)

    def copy_b(q):
        return remote(send_b.at[q], recv_b.at[q], b_out.at[q], b_in.at[q], other_y)

    def copy_2a(q):
        return remote(send_2a.at[q], recv_2a.at[q], a2_out.at[q], a2_in.at[q], other_y)

    def copy_2b(q):
        return remote(send_2b.at[q], recv_2b.at[q], b2_out.at[q], b2_in.at[q], other_x)

    last = n_occ - 1

    def copy_z(p, q, way, hop, source):
        part = wholes[p].at[source, pl.ds(q * tiles, tiles)]
        target = jnp.clip(o + 1 - 2 * way, 0, last)
        return remote(
            part, part, z_out.at[way, hop, p, q], z_in.at[way, hop, p, q], s, target
        )

    def sends(way, hop):
        return (o < last) & (o >= hop) if way == 0 else (o > 0) & (o + hop <= last)

    def held(way, hop):
        return o - hop if way == 0 else o + hop

    def product(p, q, pan):
        return lax.dot_general(
            gamma[p],
            virt[q, pan],
            (((1,), (0,)), ((), ())),
            preferred_element_type=jnp.float32,
        )

    def step(it, carry):
        @pl.when(it + 1 < parts)
        def _():
            load_part(it + 1)

        @pl.when(it == parts)
        def _():
            fetch.start()

        for p in range(AUX):
            @pl.when((it >= 3 + p * parts) & (it < 3 + (p + 1) * parts))
            def _(p=p):
                ch = it - 3
                q = ch - p * parts
                copy_2a(ch).wait_recv()
                copy_2b(ch).wait_recv()
                for h, arrived in ((0, recv_2a), (1, recv_2b)):
                    total = keep_2[h] + arrived[ch].astype(jnp.float32)
                    total = total.astype(jnp.bfloat16)
                    for t in range(tiles):
                        wholes[p][o, q * tiles + t, h * quarter:(h + 1) * quarter] = total[
                            :, t * TILE:(t + 1) * TILE
                        ]

            for way in range(2):
                @pl.when(
                    (it >= 3 + p * parts) & (it < 3 + (p + 1) * parts) & sends(way, 0)
                )
                def _(p=p, way=way):
                    copy_z(p, it - 3 - p * parts, way, 0, o).start()

        @pl.when((it >= 2) & (it < chunks + 2))
        def _():
            q = it - 2
            copy_a(q).wait_recv()
            send_2a[q] = (keep_a[1] + recv_a[q, 1].astype(jnp.float32)).astype(jnp.bfloat16)
            copy_2a(q).start()
            copy_b(q).wait_recv()
            send_2b[q] = (keep_b[1] + recv_b[q, 1].astype(jnp.float32)).astype(jnp.bfloat16)
            copy_2b(q).start()
            keep_2[0] = keep_a[0] + recv_a[q, 0].astype(jnp.float32)
            keep_2[1] = keep_b[0] + recv_b[q, 0].astype(jnp.float32)

        for p in range(AUX):
            @pl.when((it >= 1 + p * parts) & (it < 1 + (p + 1) * parts))
            def _(p=p):
                ch = it - 1
                q = ch - p * parts
                if p == 0:
                    for g in range(group):
                        load(q, 2 * g + core).wait()
                copy_c(ch).wait_recv()
                for b, a in ((1, 1), (0, 1), (1, 0), (0, 0)):
                    gx = x + a - 2 * x * a
                    gy = y + b - 2 * y * b
                    g = gy * 2 + gx
                    total = product(p, q, 2 * g + core) + recv_c[ch, g].astype(jnp.float32)
                    if a:
                        send_a[ch, b] = total[:quarter].astype(jnp.bfloat16)
                    else:
                        keep_a[b] = total[:quarter]
                    if b:
                        send_b[ch, a] = total[quarter:].astype(jnp.bfloat16)
                    else:
                        keep_b[a] = total[quarter:]
                    if (b, a) == (0, 1):
                        copy_a(ch).start()
                    if (b, a) == (1, 0):
                        copy_b(ch).start()

        for p in range(AUX):
            @pl.when((it >= p * parts) & (it < (p + 1) * parts))
            def _(p=p):
                q = it - p * parts
                if p == 0:
                    for g in range(group):
                        load(q, 2 * g + 1 - core).wait()

                def one(g, c):
                    send_c[it, g] = product(p, q, 2 * g + 1 - core).astype(jnp.bfloat16)
                    return c

                lax.fori_loop(0, group, one, 0)
                copy_c(it).start()

        for hop in range(1, last):
            lag = 3 + 2 * hop
            for p in range(AUX):
                for way in range(2):
                    @pl.when(
                        (it >= lag + p * parts)
                        & (it < lag + (p + 1) * parts)
                        & sends(way, hop)
                    )
                    def _(p=p, way=way, hop=hop, lag=lag):
                        q = it - lag - p * parts
                        copy_z(p, q, way, hop - 1, held(way, hop)).wait_recv()
                        copy_z(p, q, way, hop, held(way, hop)).start()

        return carry

    lax.fori_loop(0, chunks + 3 + 2 * max(last - 1, 0), step, 0)

    fetch.wait()

    def tile_send(p, d, source, target):
        return remote(
            picked.at[p, target], out_ref.at[source, p],
            t_out.at[p, d - 1], t_in.at[p, d - 1], target,
        )

    def own(p):
        return pltpu.make_async_copy(picked.at[p, s], out_ref.at[s, p], own_sem.at[p])

    for p in range(AUX):
        for hop in range(1, n_occ):
            for way, end in ((0, last), (1, 0)):
                @pl.when(o == end)
                def _(p=p, hop=hop, way=way):
                    def arrive(q, c):
                        copy_z(p, q, way, hop - 1, held(way, hop)).wait_recv()
                        return c

                    lax.fori_loop(0, parts, arrive, 0)

        def one_owner(d, c):
            j = lax.rem(s + d, n_pan)
            for k in range(SCAP):
                row = row_of[j * SCAP + k]
                col = col_of[j * SCAP + k]
                kept = kept_of[j * SCAP + k].astype(jnp.float32)
                total = lax.dot_general(
                    coef[row],
                    jnp.concatenate(
                        [wholes[p][z, col] for z in range(n_occ)]
                    ),
                    (((1,), (0,)), ((), ())),
                    preferred_element_type=jnp.float32,
                )
                picked[p, j, k] = (total * kept).astype(jnp.bfloat16)

            @pl.when(d < n_pan)
            def _():
                tile_send(p, d, s, j).start()

            return c

        lax.fori_loop(1, n_pan + 1, one_owner, 0)
        own(p).start()

    def drain(ch, c):
        for copy in (copy_c, copy_a, copy_b, copy_2a, copy_2b):
            copy(ch).wait_send()
        return c

    lax.fori_loop(0, chunks, drain, 0)

    for p in range(AUX):
        for hop in range(last):
            for way in range(2):
                @pl.when(sends(way, hop))
                def _(p=p, hop=hop, way=way):
                    def drain_z(q, c):
                        copy_z(p, q, way, hop, held(way, hop)).wait_send()
                        return c

                    lax.fori_loop(0, parts, drain_z, 0)

        def finish(d, c):
            tile_send(p, d, s, lax.rem(s + d, n_pan)).wait_send()
            source = lax.rem(s + n_pan - d, n_pan)
            tile_send(p, d, source, source).wait_recv()
            return c

        lax.fori_loop(1, n_pan, finish, 0)
        own(p).wait()


def by_kernel(n_occ, n_pan, gamma_ia, coef_virt, coef_occ, tile_mask, tile_owner):
    half = gamma_ia.shape[1]
    depth = gamma_ia.shape[2]
    panel_width = coef_virt.shape[0] // n_pan
    row_tiles = coef_occ.shape[0] // TILE
    col_tiles = panel_width // TILE
    parts = PARTS if col_tiles % PARTS == 0 else 1
    width = panel_width // parts
    chunks = AUX * parts
    group = n_pan // 2
    quarter = half // 2
    slot_tile, filled = block_slots(tile_mask, tile_owner, row_tiles, col_tiles, n_pan)
    flat_slots = slot_tile.reshape(-1)
    bf16, f32 = jnp.bfloat16, jnp.float32
    dma = pltpu.SemaphoreType.DMA
    smem = pl.BlockSpec(memory_space=pltpu.SMEM)
    hbm = pl.BlockSpec(memory_space=pl.ANY)
    arrived = pl.pallas_call(
        functools.partial(kernel, n_occ, n_pan, parts),
        out_shape=jax.ShapeDtypeStruct((n_pan, AUX, SCAP, TILE, TILE), bf16),
        in_specs=[smem, smem, smem, pl.BlockSpec(memory_space=pltpu.VMEM), hbm, hbm],
        out_specs=hbm,
        scratch_shapes=[
            pltpu.VMEM((AUX, half, depth), bf16),
            pltpu.VMEM((parts, n_pan, depth, width), bf16),
            pltpu.VMEM((row_tiles, TILE, coef_occ.shape[1]), bf16),
            pltpu.VMEM((chunks, group, half, width), bf16),
            pltpu.VMEM((chunks, group, half, width), bf16),
            pltpu.VMEM((2, quarter, width), f32),
            pltpu.VMEM((2, quarter, width), f32),
            pltpu.VMEM((chunks, 2, quarter, width), bf16),
            pltpu.VMEM((chunks, 2, quarter, width), bf16),
            pltpu.VMEM((chunks, 2, quarter, width), bf16),
            pltpu.VMEM((chunks, 2, quarter, width), bf16),
            pltpu.VMEM((2, quarter, width), f32),
            pltpu.VMEM((chunks, quarter, width), bf16),
            pltpu.VMEM((chunks, quarter, width), bf16),
            pltpu.VMEM((chunks, quarter, width), bf16),
            pltpu.VMEM((chunks, quarter, width), bf16),
            pltpu.VMEM((n_occ, col_tiles, half, TILE), bf16),
            pltpu.VMEM((n_occ, col_tiles, half, TILE), bf16),
            pltpu.VMEM((AUX, n_pan, SCAP, TILE, TILE), bf16),
            dma((parts, n_pan)), dma, dma((AUX,)),
            *[dma((chunks,)) for _ in range(10)],
            dma((2, n_occ - 1, AUX, parts)), dma((2, n_occ - 1, AUX, parts)),
            dma((AUX, n_pan - 1)), dma((AUX, n_pan - 1)),
        ],
        compiler_params=pltpu.CompilerParams(
            collective_id=0, has_side_effects=True, vmem_limit_bytes=67043328
        ),
    )(
        flat_slots // col_tiles,
        flat_slots % col_tiles,
        filled.reshape(-1),
        jnp.swapaxes(gamma_ia, 1, 2),
        coef_virt.T,
        coef_occ.reshape(row_tiles, TILE, coef_occ.shape[1]),
    )
    return jnp.swapaxes(arrived, 1, 2)[None, None]


def solution(mesh):
    n_occ, n_pan = mesh.shape["occ"], mesh.shape["pan"]
    local = functools.partial(by_kernel, n_occ, n_pan) if n_pan == 8 else by_collectives
    return jax.shard_map(
        local,
        mesh=mesh,
        in_specs=(P(None, "occ", "pan"), P(None, "pan"), P("occ", None), P(), P()),
        out_specs=P("occ", "pan", None, None, None, None, None),
        check_vma=False,
    )
```
